32 devices in a mesh: sector: 8 (over y, x, core), slab: 4 (over z).
Axes of the slice: x: 2, y: 2, z: 4, core: 2. Of those that a mesh axis runs over, the one named last changes fastest.
Arguments:
- iterate: float32 [32, 60, 4096], P('slab', None, 'sector'), may hold values from -6 to 6
- right_side: float32 [32, 60, 4096], P('slab', None, 'sector'), may hold values from -6 to 6
- geometry: float32 [32, 3, 4096], P('slab', None, 'sector'), may hold values from 0.5 to 2
- temporal_block_scale: float32 [32, 4096], P('slab', 'sector'), may hold values from 1 to 2.1
- decay_rates: float32 [60], replicated, may hold values from 0.49 to 0.996
- neighbour_index: int32 [5, 4096], P(None, 'sector'), may hold values from 0 to 511, as said below
- neighbour_side: int32 [5, 4096], P(None, 'sector'), may hold values from -1 to 1, as said below
- orientation: int32 [5, 4096], P(None, 'sector'), may hold values from 0 to 2
- sector_counts: int32 [8], P('sector'), may hold values from 384 to 512, as said below
- volume_ops: float32 [4, 60, 60], replicated, may hold values from -0.75 to 0.75
- face_ops: float32 [5, 60, 180], replicated, may hold values from -0.75 to 0.75
- time_coupling: float32 [60, 60], replicated, may hold values from -0.75 to 0.75
- precondition: float32 [60, 60], replicated, may hold values from -0.375 to 0.375
Outputs:
- smoothed: float32 [32, 60, 4096], P('slab', None, 'sector')
- final_section_residual: float32 [32, 60, 4096], P('slab', None, 'sector')
The draws below stay inside these ranges and needn't reach their ends.
Inputs may be any that keep to these rules, and one draw needn't show every extreme that they name: `sector_counts`: each sector holds from 384 to 512 live elements; some sector is full and some holds exactly 384. `neighbour_index`: faces of live elements name live elements; the first face of a slot below 192 names a slot of 320 or more, of the preceding sector or of its own; the first face of a slot from 320 up names a slot below 192, of the following sector or of its own; all other faces stay in the sector. `neighbour_side`: only the first face of a slot below 192 or from 320 up may leave the sector.
All inputs are finite; a program needn't handle non-finite values.
Results may differ from the reference program's by a relative error of at most 0.0042.
Values may be sent and summed in bfloat16 or wider, within the bound.
A program may use at most 64 MiB of HBM per device.

```python
import math
import jax
import jax.numpy as jnp
from jax import lax

E = 512
SLABS_PER_CYCLE = 32
NDOF = 60
FACES = 5
SECTIONS = 2
B = 192
NE = 4096


def counts_law(key):
    first, second_section_pass, third = jax.random.split(jax.random.fold_in(key, 11), 3)
    sectors = NE // E
    counts = jax.random.randint(first, (sectors,), 2 * B, E + 1)
    fullest = jax.random.randint(second_section_pass, (), 0, sectors)
    emptiest = (fullest + 1 + jax.random.randint(third, (), 0, sectors - 1)) % sectors
    counts = counts.at[fullest].set(E)
    counts = counts.at[emptiest].set(2 * B)
    return counts.astype(jnp.int32)


def neighbour_law(key):
    counts = counts_law(key)
    first, second_section_pass = jax.random.split(jax.random.fold_in(key, 23))
    sectors = NE // E
    slots = jnp.arange(E, dtype=jnp.int32)
    limit = counts[:, None]
    raw = jax.random.randint(first, (FACES, sectors, E), 0, 1 << 20)
    picked = raw % limit[None]
    inside = jnp.where(picked < limit[None] - B, picked, picked - (limit[None] - B) + (E - B))
    across = jax.random.randint(second_section_pass, (sectors, E), 0, B)
    crossing = (jax.random.randint(jax.random.fold_in(key, 37), (sectors, E), 0, 4) > 0).astype(jnp.int32)
    lower = jnp.broadcast_to((slots < B)[None, :], (sectors, E))
    upper = jnp.broadcast_to((slots >= E - B)[None, :], (sectors, E))
    side_first = jnp.where(lower, -crossing, jnp.where(upper, crossing, 0)).astype(jnp.int32)
    index_first = jnp.where(lower, E - B + across, jnp.where(upper, across, inside[0]))
    sides = jnp.concatenate([side_first[None], jnp.zeros((FACES - 1, sectors, E), jnp.int32)], axis=0)
    indices = jnp.concatenate([index_first[None], inside[1:]], axis=0)
    return (sides.reshape(FACES, NE).astype(jnp.int32), indices.reshape(FACES, NE).astype(jnp.int32))


def draw_sector_counts(key, part):
    return counts_law(key)


def draw_neighbour_index(key, part):
    return neighbour_law(key)[1]


def draw_neighbour_side(key, part):
    return neighbour_law(key)[0]


def draw_temporal_block_scale(key, part):
    first, second_section_pass, third = jax.random.split(key, 3)
    base = jnp.exp(jax.random.uniform(first, (SLABS_PER_CYCLE, NE), jnp.float32, 0.0, 0.03))
    pulse_groups = jax.random.randint(second_section_pass, (3,), 0, SLABS_PER_CYCLE)
    marked_elements = jnp.any(jnp.arange(SLABS_PER_CYCLE)[:, None] == pulse_groups[None, :], axis=1)
    jump = jax.random.uniform(third, (SLABS_PER_CYCLE, NE), jnp.float32, 1.25, 2.0)
    return jnp.where(marked_elements[:, None], base * jump, base).astype(jnp.float32)


def draw_decay_rates(key, part):
    power = jax.random.uniform(key, (NDOF,), jnp.float32, -2.3, -0.3)
    return (1.0 - jnp.power(10.0, power)).astype(jnp.float32)


def touch_ends(drawn, key, smallest, largest):
    spot = [jax.random.randint(jax.random.fold_in(key, axis), (), 0, length) for axis, length in enumerate(drawn.shape)]
    widest = drawn.shape.index(max(drawn.shape))
    beside = spot[:widest] + [(spot[widest] + 1) % drawn.shape[widest]] + spot[widest + 1:]
    return drawn.at[tuple(spot)].set(smallest).at[tuple(beside)].set(largest)


def block_scale(key, extent, pieces, smallest, top_value):
    level = 1.0
    for position, parts in pieces:
        heights = jax.random.uniform(jax.random.fold_in(jax.random.fold_in(key, 6), position), (parts,), jnp.float32, smallest / len(pieces), top_value / len(pieces))
        level = level * jnp.repeat(jnp.exp(heights), extent[position] // parts).reshape((-1,) + (1,) * (len(extent) - 1 - position))
    return level


def bell_draw(own_key, shape, spread, bound, shards=(), kind=jnp.bfloat16):
    level = block_scale(own_key, shape, shards, -0.22, 0.18) if shards else 1.0
    entries = jax.random.normal(own_key, shape, jnp.float32) * spread * level
    return jnp.minimum(jnp.maximum(entries, -bound), bound).astype(kind)


def setup_inputs(seed: int = 0) -> dict:
    streams_of = jax.random.split(jax.random.key(seed), 14)
    iterate = bell_draw(streams_of[0], (SLABS_PER_CYCLE, NDOF, NE), 1.0, 6.0, ((0, 4), (2, 8)), jnp.float32)
    right_side = bell_draw(streams_of[1], (SLABS_PER_CYCLE, NDOF, NE), 1.0, 6.0, ((0, 4), (2, 8)), jnp.float32)
    geometry = jnp.clip(jnp.exp(math.log(2.0) - 1.3862944 * jax.random.uniform(streams_of[2], (SLABS_PER_CYCLE, 3, NE), jnp.float32) ** block_scale(streams_of[2], (SLABS_PER_CYCLE, 3, NE), ((0, 4), (2, 8)), -0.2, 0.2)), 0.5, 2.0)
    temporal_block_scale = draw_temporal_block_scale(jax.random.fold_in(streams_of[13], 71), 0)
    decay_rates = draw_decay_rates(jax.random.fold_in(streams_of[13], 71), 0)
    neighbour_index = draw_neighbour_index(jax.random.fold_in(streams_of[13], 71), 0)
    neighbour_side = draw_neighbour_side(jax.random.fold_in(streams_of[13], 71), 0)
    orientation = touch_ends(jax.random.randint(streams_of[7], (FACES, NE), 0, 3), jax.random.fold_in(streams_of[7], 1), 0, 2).astype(jnp.int32)
    sector_counts = draw_sector_counts(jax.random.fold_in(streams_of[13], 71), 0)
    volume_ops = bell_draw(streams_of[9], (4, NDOF, NDOF), NDOF ** -0.5, 0.75, (), jnp.float32)
    face_ops = bell_draw(streams_of[10], (FACES, NDOF, 3 * NDOF), NDOF ** -0.5, 0.75, (), jnp.float32)
    time_coupling = bell_draw(streams_of[11], (NDOF, NDOF), NDOF ** -0.5, 0.75, (), jnp.float32)
    precondition = bell_draw(streams_of[12], (NDOF, NDOF), (4 * NDOF) ** -0.5, 0.375, (), jnp.float32)
    return {"iterate": iterate, "right_side": right_side, "geometry": geometry, "temporal_block_scale": temporal_block_scale, "decay_rates": decay_rates, "neighbour_index": neighbour_index, "neighbour_side": neighbour_side, "orientation": orientation, "sector_counts": sector_counts, "volume_ops": volume_ops, "face_ops": face_ops, "time_coupling": time_coupling, "precondition": precondition}


RELAX = 0.8
HIGH = lax.Precision.HIGHEST


def product(left, right):
    return jnp.dot(left, right, precision=HIGH, preferred_element_type=jnp.float32)


def cyclic_solve(source, scale, rate):
    values = lax.optimization_barrier(source).astype(jnp.float32)

    def advance(carry, items):
        state, gain = carry
        row, scale_row = items
        state = (row + rate * state) / scale_row[None, :]
        gain = gain * (rate / scale_row[None, :])
        return (state, gain), (state, gain)

    start = (jnp.zeros_like(values[0]), jnp.ones_like(values[0]))
    _, (states, gains) = lax.scan(advance, start, (values, scale))
    closing = states[-1] / (1.0 - gains[-1])
    return states + gains * closing[None]


def reference(iterate, right_side, geometry, temporal_block_scale, decay_rates, neighbour_index, neighbour_side, orientation, sector_counts, volume_ops, face_ops, time_coupling, precondition):
    sectors = NE // E
    slots = jnp.arange(E, dtype=jnp.int32)
    live = ((slots[None, :] < sector_counts[:, None] - B) | (slots[None, :] >= E - B)).astype(jnp.float32).reshape(NE)
    place = jnp.where(neighbour_side == 0, B + neighbour_index, jnp.where(neighbour_side < 0, neighbour_index - (E - B), E + B + neighbour_index)).astype(jnp.int32)
    place = place.reshape(FACES, sectors, E)
    masks = [[(orientation[face_id] == rotation).astype(jnp.float32).reshape(sectors, E) for rotation in range(3)] for face_id in range(FACES)]
    rate = decay_rates[:, None]

    def single_slab_update(items):
        current, before, metric = items
        applied = product(volume_ops[0], current)
        for direction in range(3):
            applied = applied + metric[direction][None, :] * product(volume_ops[direction + 1], current)
        blocks = current.reshape(NDOF, sectors, E)
        extended = jnp.concatenate([jnp.roll(blocks, 1, axis=1)[:, :, E - B:], blocks, jnp.roll(blocks, -1, axis=1)[:, :, :B]], axis=2)
        for face_id in range(FACES):
            picked = jnp.take_along_axis(extended, place[face_id][None], axis=2)
            stacked = jnp.concatenate([picked * masks[face_id][rotation][None] for rotation in range(3)], axis=0)
            applied = applied + product(face_ops[face_id], stacked.reshape(3 * NDOF, NE))
        return applied - product(time_coupling, before)

    field = iterate
    residual = right_side
    for section_id in range(SECTIONS):
        previous = jnp.roll(field, 1, axis=0)
        applied = lax.map(single_slab_update, (field, previous, geometry))
        residual = live[None, None, :] * (right_side - applied)
        source = jnp.einsum('ij,sje->sie', precondition, residual, precision=HIGH).astype(jnp.bfloat16)
        correction = cyclic_solve(source, temporal_block_scale, rate).astype(jnp.bfloat16)
        field = field + RELAX * correction.astype(jnp.float32)
    return field, residual
```

```python
import functools

import jax
import jax.numpy as jnp
from jax import lax
from jax.experimental import pallas as pl
from jax.experimental.pallas import tpu as pltpu
from jax.sharding import PartitionSpec as P

SECTIONS = 2
RELAX = 0.8
F32 = jnp.float32
BF16 = jnp.bfloat16
MESH = pl.DeviceIdType.MESH


def dot(left, right):
    return jnp.dot(left, right, preferred_element_type=F32)


def split(value):
    high = value.astype(BF16)
    return high, (value - high.astype(F32)).astype(BF16)


def smoother(
    n_sector, n_slab, dof, row,
    iterate, right_side, geometry, scale, rates, index, side, orientation, counts,
    volume_ops, face_ops, time_coupling, precondition,
    smoothed, final_residual,
    cells, onehot, edge_onehot, picked, masks, face_f32, face_w, volume_f32, volume_w, pre_f32, pre_w,
    residual_parts, source, inverse, rate_rows, closing, state,
    before, after, previous, gain_out, gain_in, offset_out, offset_in,
    send_sems, recv_sems,
):
    slabs, _, count = iterate.shape
    faces = index.shape[0]
    half = count // 2
    width = 3 * count // 8
    my_sector, my_slab = lax.axis_index("sector"), lax.axis_index("slab")
    next_sector = lax.rem(my_sector + 1, n_sector)
    prev_sector = lax.rem(my_sector + n_sector - 1, n_sector)
    ahead = [None] + [lax.rem(my_slab + m, n_slab) for m in range(1, n_slab)]

    barrier = pltpu.get_barrier_semaphore()
    for target in (next_sector, prev_sector):
        pl.semaphore_signal(barrier, inc=1, device_id={"sector": target}, device_id_type=MESH)
    for m in range(1, n_slab):
        pl.semaphore_signal(barrier, inc=1, device_id={"slab": ahead[m]}, device_id_type=MESH)

    def remote(src, dst, slot, target):
        return pltpu.make_async_remote_copy(
            src_ref=src, dst_ref=dst, send_sem=send_sems.at[slot], recv_sem=recv_sems.at[slot],
            device_id=target, device_id_type=MESH,
        )

    per_section = 3 + n_slab - 1
    gain_base = SECTIONS * per_section

    cells[...] = jnp.zeros_like(cells)

    def to_cells(s, carry):
        cells[s + 1, 0:dof, :] = iterate[s].astype(BF16)
        return carry

    lax.fori_loop(0, slabs, to_cells, 0)
    total = 1.0 / scale[0:1, :]
    inverse[0:1, :] = total
    for s in range(1, slabs):
        one = 1.0 / scale[s : s + 1, :]
        inverse[s : s + 1, :] = one
        total = total * one
    gain_out[...] = jnp.broadcast_to(total, gain_out.shape)

    pl.semaphore_wait(barrier, 2 + n_slab - 1)

    def field_copies(section):
        base = section * per_section
        inner = cells.at[pl.ds(1, slabs)]
        return [
            remote(inner.at[:, :, pl.ds(half, half)], before.at[section], base, {"sector": next_sector}),
            remote(inner.at[:, :, pl.ds(0, half)], after.at[section], base + 1, {"sector": prev_sector}),
            remote(cells.at[slabs], previous.at[section], base + 2, {"slab": ahead[1]}),
        ]

    def offset_copies(section):
        base = section * per_section + 2
        return [
            remote(offset_out.at[section], offset_in.at[section, m], base + m, {"slab": ahead[m]})
            for m in range(1, n_slab)
        ]

    gain_copies = [
        remote(gain_out, gain_in.at[m], gain_base + m - 1, {"slab": ahead[m]}) for m in range(1, n_slab)
    ]

    field_now = field_copies(0)
    for copy in field_now:
        copy.start()
    for copy in gain_copies:
        copy.start()

    rows = lax.broadcasted_iota(jnp.int32, (count, count), 0)
    side_first = side[0:1, :]
    index_first = index[0:1, :]
    own_first = jnp.where(side_first == 0, index_first, -1)
    onehot[0] = jnp.where(rows == own_first, 1.0, 0.0).astype(BF16)

    def build(f, carry):
        onehot[f] = jnp.where(rows == index[pl.ds(f, 1), :], 1.0, 0.0).astype(BF16)
        return carry

    lax.fori_loop(1, faces, build, 0)
    edge_rows = lax.broadcasted_iota(jnp.int32, (half, half), 0)
    from_before = jnp.where(side_first < 0, index_first - half, -1)[:, 0:half]
    from_after = jnp.where(side_first > 0, index_first, -1)[:, half:count]
    edge_onehot[0] = jnp.where(edge_rows == from_before, 1.0, 0.0).astype(BF16)
    edge_onehot[1] = jnp.where(edge_rows == from_after, 1.0, 0.0).astype(BF16)
    for f in range(faces):
        turned = orientation[f : f + 1, :]
        for o in range(3):
            mask = jnp.where(turned == o, 1.0, 0.0)
            masks[3 * f + o] = jnp.broadcast_to(mask, (row, count)).astype(BF16)

    face_f32[...] = jnp.zeros_like(face_f32)
    for f in range(faces):
        for o in range(3):
            at = (3 * f + o) * row
            face_f32[0:dof, at : at + dof] = face_ops[f, :, o * dof : (o + 1) * dof]
    high, low = split(face_f32[...])
    face_w[0:row, :] = high
    face_w[row : 2 * row, :] = low
    volume_f32[...] = jnp.zeros_like(volume_f32)
    volume_f32[0:dof, 0:dof] = -time_coupling[...]
    for d in range(4):
        volume_f32[d * row : d * row + dof, row : row + dof] = volume_ops[d]
    high, low = split(volume_f32[...])
    volume_w[:, 0 : 2 * row] = high
    volume_w[:, 2 * row : 4 * row] = low
    pre_f32[...] = jnp.zeros_like(pre_f32)
    for part in range(3):
        pre_f32[0:dof, part * row : part * row + dof] = precondition[...]
    high, low = split(pre_f32[...])
    part_of = lax.broadcasted_iota(jnp.int32, pre_f32.shape, 1) // row
    pre_w[...] = jnp.where(part_of == 1, low.astype(F32), high.astype(F32)).astype(BF16)
    residual_parts[...] = jnp.zeros_like(residual_parts)

    diagonal = lax.broadcasted_iota(jnp.int32, (dof, dof), 0) == lax.broadcasted_iota(jnp.int32, (dof, dof), 1)
    column = jnp.sum(jnp.where(diagonal, jnp.broadcast_to(rates[...], (dof, dof)), 0.0), axis=1, keepdims=True)
    rate_rows[...] = jnp.broadcast_to(column, (dof, count))
    power = column
    for _ in range(slabs - 1):
        power = power * column

    slots = lax.broadcasted_iota(jnp.int32, (1, count), 1)
    live = jnp.where((slots < counts[0] - width) | (slots >= count - width), 1.0, 0.0)
    offset_out[...] = jnp.zeros_like(offset_out)

    for section in range(SECTIONS):
        last = section == SECTIONS - 1
        flat = slabs * row

        def gather(f, carry):
            values = cells[pl.ds(1, slabs)].reshape(flat, count)
            picked[f] = dot(values, onehot[f]).astype(BF16).reshape(slabs, row, count)
            return carry

        lax.fori_loop(0, faces, gather, 0)
        for copy in field_now:
            copy.wait()
        cells[0] = previous[section]
        left = dot(before[section].reshape(flat, half), edge_onehot[0]).astype(BF16)
        picked[0, :, :, 0:half] = picked[0, :, :, 0:half] + left.reshape(slabs, row, half)
        right = dot(after[section].reshape(flat, half), edge_onehot[1]).astype(BF16)
        picked[0, :, :, half:count] = picked[0, :, :, half:count] + right.reshape(slabs, row, half)

        state[...] = jnp.zeros_like(state)

        def apply(s, carry):
            pair = cells[pl.ds(s, 2)].reshape(2 * row, count)
            terms = dot(volume_w[...], jnp.concatenate([pair, pair], axis=0))
            applied = terms[0:row]
            for d in range(3):
                applied = applied + geometry[s, d : d + 1, :] * terms[(d + 1) * row : (d + 2) * row]
            blocks = []
            for f in range(faces):
                block = picked[f, s]
                for o in range(3):
                    blocks.append(block * masks[3 * f + o])
            flux = dot(face_w[...], jnp.concatenate(blocks, axis=0))
            applied = applied + flux[0:row] + flux[row : 2 * row]
            residual = live * (right_side[s] - applied[0:dof])
            if last:
                final_residual[s] = residual
            high, low = split(residual)
            residual_parts[0:dof, :] = high
            residual_parts[row : row + dof, :] = high
            residual_parts[2 * row : 2 * row + dof, :] = low
            rounded = dot(pre_w[...], residual_parts[...])[0:dof].astype(BF16)
            source[s, 0:dof, :] = rounded
            state[...] = inverse[pl.ds(s, 1), :] * (rate_rows[...] * state[...] + rounded.astype(F32))
            return carry

        lax.fori_loop(0, slabs, apply, 0)
        offset_out[section, 0:dof, :] = state[...]
        offsets = offset_copies(section)
        for copy in offsets:
            copy.start()
        if section == 0:
            for copy in gain_copies:
                copy.wait()
            whole = power * gain_out[0:1, :]
            for m in range(1, n_slab):
                whole = whole * (power * gain_in[m, 0:1, :])
            closing[...] = 1.0 / (1.0 - whole)
        for copy in offsets:
            copy.wait()
        entering = state[...]
        for m in range(n_slab - 1, 0, -1):
            entering = offset_in[section, m, 0:dof, :] + (power * gain_in[m, 0:1, :]) * entering
        state[...] = entering * closing[...]
        field = iterate if section == 0 else smoothed

        def advance(s, carry):
            value = inverse[pl.ds(s, 1), :] * (rate_rows[...] * state[...] + source[s, 0:dof, :].astype(F32))
            state[...] = value
            updated = field[s] + RELAX * value.astype(BF16).astype(F32)
            smoothed[s] = updated
            if not last:
                cells[s + 1, 0:dof, :] = updated.astype(BF16)
            return carry

        lax.fori_loop(0, slabs, advance, 0)
        if not last:
            field_now = field_copies(section + 1)
            for copy in field_now:
                copy.start()


def on_device(
    n_sector, n_slab,
    iterate, right_side, geometry, temporal_block_scale, decay_rates, neighbour_index,
    neighbour_side, orientation, sector_counts, volume_ops, face_ops, time_coupling, precondition,
):
    slabs, dof, count = iterate.shape
    faces = neighbour_index.shape[0]
    row = -(-dof // 16) * 16
    half = count // 2
    vmem = pl.BlockSpec(memory_space=pltpu.VMEM)
    smem = pl.BlockSpec(memory_space=pltpu.SMEM)
    copies = SECTIONS * (3 + n_slab - 1) + n_slab - 1
    out = jax.ShapeDtypeStruct(iterate.shape, F32)
    return pl.pallas_call(
        functools.partial(smoother, n_sector, n_slab, dof, row),
        out_shape=(out, out),
        in_specs=[vmem] * 8 + [smem] + [vmem] * 4,
        out_specs=(vmem, vmem),
        scratch_shapes=[
            pltpu.VMEM((slabs + 1, row, count), BF16),
            pltpu.VMEM((faces, count, count), BF16),
            pltpu.VMEM((2, half, half), BF16),
            pltpu.VMEM((faces, slabs, row, count), BF16),
            pltpu.VMEM((3 * faces, row, count), BF16),
            pltpu.VMEM((row, 3 * faces * row), F32),
            pltpu.VMEM((2 * row, 3 * faces * row), BF16),
            pltpu.VMEM((4 * row, 2 * row), F32),
            pltpu.VMEM((4 * row, 4 * row), BF16),
            pltpu.VMEM((row, 3 * row), F32),
            pltpu.VMEM((row, 3 * row), BF16),
            pltpu.VMEM((3 * row, count), BF16),
            pltpu.VMEM((slabs, row, count), BF16),
            pltpu.VMEM((slabs, count), F32),
            pltpu.VMEM((dof, count), F32),
            pltpu.VMEM((dof, count), F32),
            pltpu.VMEM((dof, count), F32),
            pltpu.VMEM((SECTIONS, slabs, row, half), BF16),
            pltpu.VMEM((SECTIONS, slabs, row, half), BF16),
            pltpu.VMEM((SECTIONS, row, count), BF16),
            pltpu.VMEM((8, count), F32),
            pltpu.VMEM((n_slab, 8, count), F32),
            pltpu.VMEM((SECTIONS, row, count), F32),
            pltpu.VMEM((SECTIONS, n_slab, row, count), F32),
            pltpu.SemaphoreType.DMA((copies,)),
            pltpu.SemaphoreType.DMA((copies,)),
        ],
        compiler_params=pltpu.CompilerParams(
            collective_id=0, has_side_effects=True, vmem_limit_bytes=56 << 20
        ),
    )(
        iterate, right_side, geometry, temporal_block_scale, decay_rates[None, :], neighbour_index,
        neighbour_side, orientation, sector_counts, volume_ops, face_ops, time_coupling, precondition,
    )


def solution(mesh):
    in_specs = (
        P("slab", None, "sector"),
        P("slab", None, "sector"),
        P("slab", None, "sector"),
        P("slab", "sector"),
        P(),
        P(None, "sector"),
        P(None, "sector"),
        P(None, "sector"),
        P("sector"),
        P(),
        P(),
        P(),
        P(),
    )
    out_specs = (P("slab", None, "sector"), P("slab", None, "sector"))
    body = functools.partial(on_device, mesh.shape["sector"], mesh.shape["slab"])
    return jax.shard_map(body, mesh=mesh, in_specs=in_specs, out_specs=out_specs, check_vma=False)
```

```python
import functools

import jax
import jax.numpy as jnp
from jax import lax
from jax.experimental import pallas as pl
from jax.experimental.pallas import tpu as pltpu
from jax.sharding import PartitionSpec as P

SECTIONS = 2
RELAX = 0.8
LANES = 128
F32 = jnp.float32
BF16 = jnp.bfloat16
MESH = pl.DeviceIdType.MESH


def dot(left, right):
    return jnp.dot(left, right, preferred_element_type=F32)


def split(value):
    high = value.astype(BF16)
    return high, (value - high.astype(F32)).astype(BF16)


def smoother(
    n_sector, n_slab, slabs, dof, row,
    iterate, right_side, geometry, scale, rates, index, side, orientation, counts,
    volume_ops, face_ops, time_coupling, precondition,
    smoothed, final_residual,
    cells, cells_low, onehot, edge_onehot, picked, picked_low, masks, face_f32, face_w, volume_f32, volume_w, pre_f32, pre_w,
    residual_parts, source, inverse, rate_rows, closing, state,
    before, after, previous, gain_out, gain_in, offset_out, offset_in,
    send_sems, recv_sems,
):
    count = index.shape[1]
    tiles = count // LANES
    faces = index.shape[0]
    half = count // 2
    width = 3 * count // 8
    my_sector, my_slab = lax.axis_index("sector"), lax.axis_index("slab")
    next_sector = lax.rem(my_sector + 1, n_sector)
    prev_sector = lax.rem(my_sector + n_sector - 1, n_sector)
    ahead = [None] + [lax.rem(my_slab + m, n_slab) for m in range(1, n_slab)]

    barrier = pltpu.get_barrier_semaphore()
    for target in (next_sector, prev_sector):
        pl.semaphore_signal(barrier, inc=1, device_id={"sector": target}, device_id_type=MESH)
    for m in range(1, n_slab):
        pl.semaphore_signal(barrier, inc=1, device_id={"slab": ahead[m]}, device_id_type=MESH)

    def remote(src, dst, slot, target):
        return pltpu.make_async_remote_copy(
            src_ref=src, dst_ref=dst, send_sem=send_sems.at[slot], recv_sem=recv_sems.at[slot],
            device_id=target, device_id_type=MESH,
        )

    per_section = 3 + n_slab - 1
    gain_base = SECTIONS * per_section

    cells[...] = jnp.zeros_like(cells)
    cells_low[...] = jnp.zeros_like(cells_low)

    def lines(s, tile):
        return pl.ds(tile * slabs + s, dof, stride=tiles * slabs), slice(None)

    def load_slab(ref, s):
        return jnp.concatenate([ref[lines(s, tile)] for tile in range(tiles)], axis=1)

    def store_slab(ref, s, value):
        for tile in range(tiles):
            ref[lines(s, tile)] = value[:, tile * LANES : (tile + 1) * LANES]

    def to_cells(s, carry):
        high, low = split(load_slab(iterate, s))
        cells[s + 1, 0:dof, :] = high
        cells_low[s + 1, 0:dof, :] = low
        return carry

    lax.fori_loop(0, slabs, to_cells, 0)
    total = 1.0 / scale[0:1, :]
    inverse[0:1, :] = total
    for s in range(1, slabs):
        one = 1.0 / scale[s : s + 1, :]
        inverse[s : s + 1, :] = one
        total = total * one
    gain_out[...] = jnp.broadcast_to(total, gain_out.shape)

    pl.semaphore_wait(barrier, 2 + n_slab - 1)

    def field_copies(section):
        base = section * per_section
        inner = cells.at[pl.ds(1, slabs)]
        return [
            remote(inner.at[:, :, pl.ds(half, half)], before.at[section], base, {"sector": next_sector}),
            remote(inner.at[:, :, pl.ds(0, half)], after.at[section], base + 1, {"sector": prev_sector}),
            remote(cells.at[slabs], previous.at[section], base + 2, {"slab": ahead[1]}),
        ]

    def offset_copies(section):
        base = section * per_section + 2
        return [
            remote(offset_out.at[section], offset_in.at[section, m], base + m, {"slab": ahead[m]})
            for m in range(1, n_slab)
        ]

    gain_copies = [
        remote(gain_out, gain_in.at[m], gain_base + m - 1, {"slab": ahead[m]}) for m in range(1, n_slab)
    ]

    field_now = field_copies(0)
    for copy in field_now:
        copy.start()
    for copy in gain_copies:
        copy.start()

    rows = lax.broadcasted_iota(jnp.int32, (count, count), 0)
    side_first = side[0:1, :]
    index_first = index[0:1, :]
    own_first = jnp.where(side_first == 0, index_first, -1)
    onehot[0] = jnp.where(rows == own_first, 1.0, 0.0).astype(BF16)

    def build(f, carry):
        onehot[f] = jnp.where(rows == index[pl.ds(f, 1), :], 1.0, 0.0).astype(BF16)
        return carry

    lax.fori_loop(1, faces, build, 0)
    edge_rows = lax.broadcasted_iota(jnp.int32, (half, half), 0)
    from_before = jnp.where(side_first < 0, index_first - half, -1)[:, 0:half]
    from_after = jnp.where(side_first > 0, index_first, -1)[:, half:count]
    edge_onehot[0] = jnp.where(edge_rows == from_before, 1.0, 0.0).astype(BF16)
    edge_onehot[1] = jnp.where(edge_rows == from_after, 1.0, 0.0).astype(BF16)
    for f in range(faces):
        turned = orientation[f : f + 1, :]
        for o in range(3):
            mask = jnp.where(turned == o, 1.0, 0.0)
            masks[3 * f + o] = jnp.broadcast_to(mask, (row, count)).astype(BF16)

    face_f32[...] = jnp.zeros_like(face_f32)
    for f in range(faces):
        for o in range(3):
            at = (3 * f + o) * row
            face_f32[0:dof, at : at + dof] = face_ops[f, :, o * dof : (o + 1) * dof]
    high, low = split(face_f32[...])
    face_w[0:row, :] = high
    face_w[row : 2 * row, :] = low
    volume_f32[...] = jnp.zeros_like(volume_f32)
    volume_f32[0:dof, 0:dof] = -time_coupling[...]
    for d in range(4):
        volume_f32[d * row : d * row + dof, row : row + dof] = volume_ops[:, d, :]
    high, low = split(volume_f32[...])
    volume_w[:, 0 : 2 * row] = high
    volume_w[:, 2 * row : 4 * row] = low
    volume_w[:, 4 * row : 6 * row] = high
    pre_f32[...] = jnp.zeros_like(pre_f32)
    for part in range(3):
        pre_f32[0:dof, part * row : part * row + dof] = precondition[...]
    high, low = split(pre_f32[...])
    part_of = lax.broadcasted_iota(jnp.int32, pre_f32.shape, 1) // row
    pre_w[...] = jnp.where(part_of == 1, low.astype(F32), high.astype(F32)).astype(BF16)
    residual_parts[...] = jnp.zeros_like(residual_parts)

    diagonal = lax.broadcasted_iota(jnp.int32, (dof, dof), 0) == lax.broadcasted_iota(jnp.int32, (dof, dof), 1)
    column = jnp.sum(jnp.where(diagonal, jnp.broadcast_to(rates[...], (dof, dof)), 0.0), axis=1, keepdims=True)
    rate_rows[...] = jnp.broadcast_to(column, (dof, count))
    power = column
    for _ in range(slabs - 1):
        power = power * column

    slots = lax.broadcasted_iota(jnp.int32, (1, count), 1)
    live = jnp.where((slots < counts[0] - width) | (slots >= count - width), 1.0, 0.0)
    offset_out[...] = jnp.zeros_like(offset_out)

    for section in range(SECTIONS):
        last = section == SECTIONS - 1
        flat = slabs * row

        def gather(f, carry):
            values = cells[pl.ds(1, slabs)].reshape(flat, count)
            picked[f] = dot(values, onehot[f]).astype(BF16).reshape(slabs, row, count)
            values = cells_low[pl.ds(1, slabs)].reshape(flat, count)
            picked_low[f] = dot(values, onehot[f]).astype(BF16).reshape(slabs, row, count)
            return carry

        lax.fori_loop(0, faces, gather, 0)
        for copy in field_now:
            copy.wait()
        cells[0] = previous[section]
        left = dot(before[section].reshape(flat, half), edge_onehot[0]).astype(BF16)
        picked[0, :, :, 0:half] = picked[0, :, :, 0:half] + left.reshape(slabs, row, half)
        right = dot(after[section].reshape(flat, half), edge_onehot[1]).astype(BF16)
        picked[0, :, :, half:count] = picked[0, :, :, half:count] + right.reshape(slabs, row, half)

        state[...] = jnp.zeros_like(state)

        def apply(s, carry):
            pair = cells[pl.ds(s, 2)].reshape(2 * row, count)
            pair_low = cells_low[pl.ds(s, 2)].reshape(2 * row, count)
            terms = dot(volume_w[...], jnp.concatenate([pair, pair, pair_low], axis=0))
            applied = terms[0:row]
            for d in range(3):
                applied = applied + geometry[d, pl.ds(s, 1), :] * terms[(d + 1) * row : (d + 2) * row]
            blocks, blocks_low = [], []
            for f in range(faces):
                block, block_low = picked[f, s], picked_low[f, s]
                for o in range(3):
                    blocks.append(block * masks[3 * f + o])
                    blocks_low.append(block_low * masks[3 * f + o])
            flux = dot(face_w[...], jnp.concatenate(blocks, axis=0))
            flux_low = dot(face_w[0:row, :], jnp.concatenate(blocks_low, axis=0))
            applied = applied + flux[0:row] + flux[row : 2 * row] + flux_low
            residual = live * (load_slab(right_side, s) - applied[0:dof])
            if last:
                store_slab(final_residual, s, residual)
            high, low = split(residual)
            residual_parts[0:dof, :] = high
            residual_parts[row : row + dof, :] = high
            residual_parts[2 * row : 2 * row + dof, :] = low
            rounded = dot(pre_w[...], residual_parts[...])[0:dof].astype(BF16)
            source[s, 0:dof, :] = rounded
            state[...] = inverse[pl.ds(s, 1), :] * (rate_rows[...] * state[...] + rounded.astype(F32))
            return carry

        lax.fori_loop(0, slabs, apply, 0)
        offset_out[section, 0:dof, :] = state[...].astype(BF16)
        offsets = offset_copies(section)
        for copy in offsets:
            copy.start()
        if section == 0:
            for copy in gain_copies:
                copy.wait()
            whole = power * gain_out[0:1, :]
            for m in range(1, n_slab):
                whole = whole * (power * gain_in[m, 0:1, :])
            closing[...] = 1.0 / (1.0 - whole)
        for copy in offsets:
            copy.wait()
        entering = state[...]
        for m in range(n_slab - 1, 0, -1):
            entering = offset_in[section, m, 0:dof, :].astype(F32) + (power * gain_in[m, 0:1, :]) * entering
        state[...] = entering * closing[...]
        field = iterate if section == 0 else smoothed

        def advance(s, carry):
            value = inverse[pl.ds(s, 1), :] * (rate_rows[...] * state[...] + source[s, 0:dof, :].astype(F32))
            state[...] = value
            updated = load_slab(field, s) + RELAX * value.astype(BF16).astype(F32)
            store_slab(smoothed, s, updated)
            if not last:
                high, low = split(updated)
                cells[s + 1, 0:dof, :] = high
                cells_low[s + 1, 0:dof, :] = low
            return carry

        lax.fori_loop(0, slabs, advance, 0)
        if not last:
            field_now = field_copies(section + 1)
            for copy in field_now:
                copy.start()


def on_device(
    n_sector, n_slab,
    iterate, right_side, geometry, temporal_block_scale, decay_rates, neighbour_index,
    neighbour_side, orientation, sector_counts, volume_ops, face_ops, time_coupling, precondition,
):
    slabs, dof, count = iterate.shape
    faces = neighbour_index.shape[0]
    row = -(-dof // 16) * 16
    half = count // 2
    tiles = count // LANES
    vmem = pl.BlockSpec(memory_space=pltpu.VMEM)
    smem = pl.BlockSpec(memory_space=pltpu.SMEM)
    copies = SECTIONS * (3 + n_slab - 1) + n_slab - 1

    def by_dof(value):
        lined = value.transpose(1, 0, 2).reshape(dof, slabs, tiles, LANES)
        return lined.transpose(0, 2, 1, 3).reshape(dof * tiles * slabs, LANES)

    def by_slab(value):
        lined = value.reshape(dof, tiles, slabs, LANES).transpose(0, 2, 1, 3)
        return lined.reshape(dof, slabs, count).transpose(1, 0, 2)

    out = jax.ShapeDtypeStruct((dof * tiles * slabs, LANES), F32)
    results = pl.pallas_call(
        functools.partial(smoother, n_sector, n_slab, slabs, dof, row),
        out_shape=(out, out),
        in_specs=[vmem] * 8 + [smem] + [vmem] * 4,
        out_specs=(vmem, vmem),
        scratch_shapes=[
            pltpu.VMEM((slabs + 1, row, count), BF16),
            pltpu.VMEM((slabs + 1, row, count), BF16),
            pltpu.VMEM((faces, count, count), BF16),
            pltpu.VMEM((2, half, half), BF16),
            pltpu.VMEM((faces, slabs, row, count), BF16),
            pltpu.VMEM((faces, slabs, row, count), BF16),
            pltpu.VMEM((3 * faces, row, count), BF16),
            pltpu.VMEM((row, 3 * faces * row), F32),
            pltpu.VMEM((2 * row, 3 * faces * row), BF16),
            pltpu.VMEM((4 * row, 2 * row), F32),
            pltpu.VMEM((4 * row, 6 * row), BF16),
            pltpu.VMEM((row, 3 * row), F32),
            pltpu.VMEM((row, 3 * row), BF16),
            pltpu.VMEM((3 * row, count), BF16),
            pltpu.VMEM((slabs, row, count), BF16),
            pltpu.VMEM((slabs, count), F32),
            pltpu.VMEM((dof, count), F32),
            pltpu.VMEM((dof, count), F32),
            pltpu.VMEM((dof, count), F32),
            pltpu.VMEM((SECTIONS, slabs, row, half), BF16),
            pltpu.VMEM((SECTIONS, slabs, row, half), BF16),
            pltpu.VMEM((SECTIONS, row, count), BF16),
            pltpu.VMEM((8, count), F32),
            pltpu.VMEM((n_slab, 8, count), F32),
            pltpu.VMEM((SECTIONS, row, count), BF16),
            pltpu.VMEM((SECTIONS, n_slab, row, count), BF16),
            pltpu.SemaphoreType.DMA((copies,)),
            pltpu.SemaphoreType.DMA((copies,)),
        ],
        compiler_params=pltpu.CompilerParams(
            collective_id=0, has_side_effects=True, vmem_limit_bytes=56 << 20
        ),
    )(
        by_dof(iterate), by_dof(right_side), geometry.transpose(1, 0, 2), temporal_block_scale,
        decay_rates[None, :], neighbour_index, neighbour_side, orientation, sector_counts,
        volume_ops.transpose(1, 0, 2), face_ops, time_coupling, precondition,
    )
    return tuple(by_slab(value) for value in results)


def solution(mesh):
    in_specs = (
        P("slab", None, "sector"),
        P("slab", None, "sector"),
        P("slab", None, "sector"),
        P("slab", "sector"),
        P(),
        P(None, "sector"),
        P(None, "sector"),
        P(None, "sector"),
        P("sector"),
        P(),
        P(),
        P(),
        P(),
    )
    out_specs = (P("slab", None, "sector"), P("slab", None, "sector"))
    body = functools.partial(on_device, mesh.shape["sector"], mesh.shape["slab"])
    return jax.shard_map(body, mesh=mesh, in_specs=in_specs, out_specs=out_specs, check_vma=False)
```

```python
import functools

import jax
import jax.numpy as jnp
from jax import lax
from jax.experimental import pallas as pl
from jax.experimental.pallas import tpu as pltpu
from jax.sharding import PartitionSpec as P

SECTIONS = 2
RELAX = 0.8
LANES = 128
F32 = jnp.float32
BF16 = jnp.bfloat16
MESH = pl.DeviceIdType.MESH


def dot(left, right):
    return jnp.dot(left, right, preferred_element_type=F32)


def split(value):
    high = value.astype(BF16)
    return high, (value - high.astype(F32)).astype(BF16)


def smoother(
    n_sector, n_slab, slabs, dof, row,
    iterate, right_side, geometry, scale, rates, index, side, orientation, counts,
    volume_ops, face_ops, time_coupling, precondition,
    smoothed, final_residual,
    cells, cells_low, onehot, edge_onehot, picked, picked_low, partial, edge, masks, face_f32, face_w, volume_f32, volume_w, pre_f32, pre_w,
    residual_parts, source, inverse, rate_rows, closing, state,
    before, after, previous, gain_out, gain_in, offset_out, offset_in,
    send_sems, recv_sems,
):
    count = index.shape[1]
    tiles = count // LANES
    faces = index.shape[0]
    half = count // 2
    width = 3 * count // 8
    my_sector, my_slab = lax.axis_index("sector"), lax.axis_index("slab")
    next_sector = lax.rem(my_sector + 1, n_sector)
    prev_sector = lax.rem(my_sector + n_sector - 1, n_sector)
    ahead = [None] + [lax.rem(my_slab + m, n_slab) for m in range(1, n_slab)]

    barrier = pltpu.get_barrier_semaphore()
    for target in (next_sector, prev_sector):
        pl.semaphore_signal(barrier, inc=1, device_id={"sector": target}, device_id_type=MESH)
    for m in range(1, n_slab):
        pl.semaphore_signal(barrier, inc=1, device_id={"slab": ahead[m]}, device_id_type=MESH)

    def remote(src, dst, slot, target):
        return pltpu.make_async_remote_copy(
            src_ref=src, dst_ref=dst, send_sem=send_sems.at[slot], recv_sem=recv_sems.at[slot],
            device_id=target, device_id_type=MESH,
        )

    per_section = 3 + 2 * (n_slab - 1)
    gain_base = SECTIONS * per_section

    cells[...] = jnp.zeros_like(cells)
    cells_low[...] = jnp.zeros_like(cells_low)

    def lines(s, tile):
        return pl.ds(tile * slabs + s, dof, stride=tiles * slabs), slice(None)

    def load_slab(ref, s, first, stop):
        return jnp.concatenate([ref[lines(s, tile)] for tile in range(first, stop)], axis=1)

    def store_slab(ref, s, value, first):
        for tile in range(value.shape[1] // LANES):
            ref[lines(s, first + tile)] = value[:, tile * LANES : (tile + 1) * LANES]

    def to_cells(s, carry):
        high, low = split(load_slab(iterate, s, 0, tiles))
        cells[s + 1, 0:dof, :] = high
        cells_low[s + 1, 0:dof, :] = low
        return carry

    lax.fori_loop(0, slabs, to_cells, 0)
    total = 1.0 / scale[0:1, :]
    inverse[0:1, :] = total
    for s in range(1, slabs):
        one = 1.0 / scale[s : s + 1, :]
        inverse[s : s + 1, :] = one
        total = total * one
    gain_out[...] = jnp.broadcast_to(total, gain_out.shape)

    pl.semaphore_wait(barrier, 2 + n_slab - 1)

    def field_copies(section):
        base = section * per_section
        inner = cells.at[pl.ds(1, slabs)]
        return [
            remote(inner.at[:, :, pl.ds(half, half)], before.at[section], base, {"sector": next_sector}),
            remote(inner.at[:, :, pl.ds(0, half)], after.at[section], base + 1, {"sector": prev_sector}),
            remote(cells.at[slabs], previous.at[section], base + 2, {"slab": ahead[1]}),
        ]

    def offset_copies(section, part):
        base = section * per_section + 2 + part * (n_slab - 1)
        return [
            remote(offset_out.at[section, part], offset_in.at[section, part, m], base + m, {"slab": ahead[m]})
            for m in range(1, n_slab)
        ]

    gain_copies = [
        remote(gain_out, gain_in.at[m], gain_base + m - 1, {"slab": ahead[m]}) for m in range(1, n_slab)
    ]

    field_now = field_copies(0)
    for copy in field_now:
        copy.start()
    for copy in gain_copies:
        copy.start()

    rows = lax.broadcasted_iota(jnp.int32, (count, count), 0)
    side_first = side[0:1, :]
    index_first = index[0:1, :]
    own_first = jnp.where(side_first == 0, index_first, -1)
    onehot[0] = jnp.where(rows == own_first, 1.0, 0.0).astype(BF16)

    def build(f, carry):
        onehot[f] = jnp.where(rows == index[pl.ds(f, 1), :], 1.0, 0.0).astype(BF16)
        return carry

    lax.fori_loop(1, faces, build, 0)
    edge_rows = lax.broadcasted_iota(jnp.int32, (half, half), 0)
    from_before = jnp.where(side_first < 0, index_first - half, -1)[:, 0:half]
    from_after = jnp.where(side_first > 0, index_first, -1)[:, half:count]
    edge_onehot[0] = jnp.where(edge_rows == from_before, 1.0, 0.0).astype(BF16)
    edge_onehot[1] = jnp.where(edge_rows == from_after, 1.0, 0.0).astype(BF16)
    for f in range(faces):
        turned = orientation[f : f + 1, :]
        for o in range(3):
            mask = jnp.where(turned == o, 1.0, 0.0)
            masks[3 * f + o] = jnp.broadcast_to(mask, (row, count)).astype(BF16)

    face_f32[...] = jnp.zeros_like(face_f32)
    for f in range(faces):
        for o in range(3):
            at = (3 * f + o) * row
            face_f32[0:dof, at : at + dof] = face_ops[f, :, o * dof : (o + 1) * dof]
    high, low = split(face_f32[...])
    face_w[0:row, :] = high
    face_w[row : 2 * row, :] = low
    volume_f32[...] = jnp.zeros_like(volume_f32)
    volume_f32[0:dof, 0:dof] = -time_coupling[...]
    for d in range(4):
        volume_f32[d * row : d * row + dof, row : row + dof] = volume_ops[:, d, :]
    high, low = split(volume_f32[...])
    volume_w[:, 0 : 2 * row] = high
    volume_w[:, 2 * row : 4 * row] = low
    volume_w[:, 4 * row : 6 * row] = high
    pre_f32[...] = jnp.zeros_like(pre_f32)
    for part in range(3):
        pre_f32[0:dof, part * row : part * row + dof] = precondition[...]
    high, low = split(pre_f32[...])
    part_of = lax.broadcasted_iota(jnp.int32, pre_f32.shape, 1) // row
    pre_w[...] = jnp.where(part_of == 1, low.astype(F32), high.astype(F32)).astype(BF16)
    residual_parts[...] = jnp.zeros_like(residual_parts)

    diagonal = lax.broadcasted_iota(jnp.int32, (dof, dof), 0) == lax.broadcasted_iota(jnp.int32, (dof, dof), 1)
    column = jnp.sum(jnp.where(diagonal, jnp.broadcast_to(rates[...], (dof, dof)), 0.0), axis=1, keepdims=True)
    rate_rows[...] = jnp.broadcast_to(column, (dof, count))
    power = column
    for _ in range(slabs - 1):
        power = power * column

    slots = lax.broadcasted_iota(jnp.int32, (1, count), 1)
    live = jnp.where((slots < counts[0] - width) | (slots >= count - width), 1.0, 0.0)
    offset_out[...] = jnp.zeros_like(offset_out)

    for section in range(SECTIONS):
        last = section == SECTIONS - 1
        flat = slabs * row

        def gather(f, carry):
            values = cells[pl.ds(1, slabs)].reshape(flat, count)
            picked[f] = dot(values, onehot[f]).astype(BF16).reshape(slabs, row, count)
            values = cells_low[pl.ds(1, slabs)].reshape(flat, count)
            picked_low[f] = dot(values, onehot[f]).astype(BF16).reshape(slabs, row, count)
            return carry

        lax.fori_loop(0, faces, gather, 0)
        cells[0] = jnp.zeros_like(cells[0])

        def apply(s, carry):
            pair = cells[pl.ds(s, 2)].reshape(2 * row, count)
            pair_low = cells_low[pl.ds(s, 2)].reshape(2 * row, count)
            terms = dot(volume_w[...], jnp.concatenate([pair, pair, pair_low], axis=0))
            applied = terms[0:row]
            for d in range(3):
                applied = applied + geometry[d, pl.ds(s, 1), :] * terms[(d + 1) * row : (d + 2) * row]
            blocks, blocks_low = [], []
            for f in range(faces):
                block, block_low = picked[f, s], picked_low[f, s]
                for o in range(3):
                    blocks.append(block * masks[3 * f + o])
                    blocks_low.append(block_low * masks[3 * f + o])
            flux = dot(face_w[...], jnp.concatenate(blocks, axis=0))
            flux_low = dot(face_w[0:row, :], jnp.concatenate(blocks_low, axis=0))
            partial[s] = applied + flux[0:row] + flux[row : 2 * row] + flux_low
            return carry

        lax.fori_loop(0, slabs, apply, 0)
        for copy in field_now:
            copy.wait()
        slab_before = previous[section]
        weights = jnp.concatenate([volume_w[0:row, 0:row], volume_w[0:row, 2 * row : 3 * row]], axis=1)
        partial[0] = partial[0] + dot(weights, jnp.concatenate([slab_before, slab_before], axis=0))
        left = dot(before[section].reshape(flat, half), edge_onehot[0]).astype(BF16)
        edge[:, :, 0:half] = left.reshape(slabs, row, half)
        right = dot(after[section].reshape(flat, half), edge_onehot[1]).astype(BF16)
        edge[:, :, half:count] = right.reshape(slabs, row, half)
        state[...] = jnp.zeros_like(state)

        offsets = []
        for part in range(2):
            lanes = slice(part * half, (part + 1) * half)
            first, stop = part * tiles // 2, (part + 1) * tiles // 2

            def finish(s, carry):
                block = edge[s, :, lanes]
                crossing = jnp.concatenate([block * masks[o, :, lanes] for o in range(3)], axis=0)
                flux = dot(face_w[:, 0 : 3 * row], crossing)
                applied = partial[s, :, lanes] + flux[0:row] + flux[row : 2 * row]
                residual = live[:, lanes] * (load_slab(right_side, s, first, stop) - applied[0:dof])
                if last:
                    store_slab(final_residual, s, residual, first)
                high, low = split(residual)
                residual_parts[0:dof, lanes] = high
                residual_parts[row : row + dof, lanes] = high
                residual_parts[2 * row : 2 * row + dof, lanes] = low
                rounded = dot(pre_w[...], residual_parts[:, lanes])[0:dof].astype(BF16)
                source[s, 0:dof, lanes] = rounded
                state[:, lanes] = inverse[pl.ds(s, 1), lanes] * (
                    rate_rows[:, lanes] * state[:, lanes] + rounded.astype(F32)
                )
                return carry

            lax.fori_loop(0, slabs, finish, 0)
            offset_out[section, part, 0:dof, :] = state[:, lanes].astype(BF16)
            offsets.append(offset_copies(section, part))
            for copy in offsets[part]:
                copy.start()
        if section == 0:
            for copy in gain_copies:
                copy.wait()
            whole = power * gain_out[0:1, :]
            for m in range(1, n_slab):
                whole = whole * (power * gain_in[m, 0:1, :])
            closing[...] = 1.0 / (1.0 - whole)
        field = iterate if section == 0 else smoothed
        if not last:
            field_now = field_copies(section + 1)
        for part in range(2):
            lanes = slice(part * half, (part + 1) * half)
            first, stop = part * tiles // 2, (part + 1) * tiles // 2
            for copy in offsets[part]:
                copy.wait()
            entering = state[:, lanes]
            for m in range(n_slab - 1, 0, -1):
                gain = power * gain_in[m, 0:1, lanes]
                entering = offset_in[section, part, m, 0:dof, :].astype(F32) + gain * entering
            state[:, lanes] = entering * closing[:, lanes]

            def advance(s, carry):
                value = inverse[pl.ds(s, 1), lanes] * (
                    rate_rows[:, lanes] * state[:, lanes] + source[s, 0:dof, lanes].astype(F32)
                )
                state[:, lanes] = value
                updated = load_slab(field, s, first, stop) + RELAX * value.astype(BF16).astype(F32)
                store_slab(smoothed, s, updated, first)
                if not last:
                    high, low = split(updated)
                    cells[s + 1, 0:dof, lanes] = high
                    cells_low[s + 1, 0:dof, lanes] = low
                return carry

            lax.fori_loop(0, slabs, advance, 0)
            if not last:
                for copy in ([field_now[1]] if part == 0 else [field_now[0], field_now[2]]):
                    copy.start()


def on_device(
    n_sector, n_slab,
    iterate, right_side, geometry, temporal_block_scale, decay_rates, neighbour_index,
    neighbour_side, orientation, sector_counts, volume_ops, face_ops, time_coupling, precondition,
):
    slabs, dof, count = iterate.shape
    faces = neighbour_index.shape[0]
    row = -(-dof // 16) * 16
    half = count // 2
    tiles = count // LANES
    vmem = pl.BlockSpec(memory_space=pltpu.VMEM)
    smem = pl.BlockSpec(memory_space=pltpu.SMEM)
    copies = SECTIONS * (3 + 2 * (n_slab - 1)) + n_slab - 1

    def by_dof(value):
        lined = value.transpose(1, 0, 2).reshape(dof, slabs, tiles, LANES)
        return lined.transpose(0, 2, 1, 3).reshape(dof * tiles * slabs, LANES)

    def by_slab(value):
        lined = value.reshape(dof, tiles, slabs, LANES).transpose(0, 2, 1, 3)
        return lined.reshape(dof, slabs, count).transpose(1, 0, 2)

    out = jax.ShapeDtypeStruct((dof * tiles * slabs, LANES), F32)
    results = pl.pallas_call(
        functools.partial(smoother, n_sector, n_slab, slabs, dof, row),
        out_shape=(out, out),
        in_specs=[vmem] * 8 + [smem] + [vmem] * 4,
        out_specs=(vmem, vmem),
        scratch_shapes=[
            pltpu.VMEM((slabs + 1, row, count), BF16),
            pltpu.VMEM((slabs + 1, row, count), BF16),
            pltpu.VMEM((faces, count, count), BF16),
            pltpu.VMEM((2, half, half), BF16),
            pltpu.VMEM((faces, slabs, row, count), BF16),
            pltpu.VMEM((faces, slabs, row, count), BF16),
            pltpu.VMEM((slabs, row, count), F32),
            pltpu.VMEM((slabs, row, count), BF16),
            pltpu.VMEM((3 * faces, row, count), BF16),
            pltpu.VMEM((row, 3 * faces * row), F32),
            pltpu.VMEM((2 * row, 3 * faces * row), BF16),
            pltpu.VMEM((4 * row, 2 * row), F32),
            pltpu.VMEM((4 * row, 6 * row), BF16),
            pltpu.VMEM((row, 3 * row), F32),
            pltpu.VMEM((row, 3 * row), BF16),
            pltpu.VMEM((3 * row, count), BF16),
            pltpu.VMEM((slabs, row, count), BF16),
            pltpu.VMEM((slabs, count), F32),
            pltpu.VMEM((dof, count), F32),
            pltpu.VMEM((dof, count), F32),
            pltpu.VMEM((dof, count), F32),
            pltpu.VMEM((SECTIONS, slabs, row, half), BF16),
            pltpu.VMEM((SECTIONS, slabs, row, half), BF16),
            pltpu.VMEM((SECTIONS, row, count), BF16),
            pltpu.VMEM((8, count), F32),
            pltpu.VMEM((n_slab, 8, count), F32),
            pltpu.VMEM((SECTIONS, 2, row, half), BF16),
            pltpu.VMEM((SECTIONS, 2, n_slab, row, half), BF16),
            pltpu.SemaphoreType.DMA((copies,)),
            pltpu.SemaphoreType.DMA((copies,)),
        ],
        compiler_params=pltpu.CompilerParams(
            collective_id=0, has_side_effects=True, vmem_limit_bytes=56 << 20
        ),
    )(
        by_dof(iterate), by_dof(right_side), geometry.transpose(1, 0, 2), temporal_block_scale,
        decay_rates[None, :], neighbour_index, neighbour_side, orientation, sector_counts,
        volume_ops.transpose(1, 0, 2), face_ops, time_coupling, precondition,
    )
    return tuple(by_slab(value) for value in results)


def solution(mesh):
    in_specs = (
        P("slab", None, "sector"),
        P("slab", None, "sector"),
        P("slab", None, "sector"),
        P("slab", "sector"),
        P(),
        P(None, "sector"),
        P(None, "sector"),
        P(None, "sector"),
        P("sector"),
        P(),
        P(),
        P(),
        P(),
    )
    out_specs = (P("slab", None, "sector"), P("slab", None, "sector"))
    body = functools.partial(on_device, mesh.shape["sector"], mesh.shape["slab"])
    return jax.shard_map(body, mesh=mesh, in_specs=in_specs, out_specs=out_specs, check_vma=False)
```

```python
import functools

import jax
import jax.numpy as jnp
from jax import lax
from jax.experimental import pallas as pl
from jax.experimental.pallas import tpu as pltpu
from jax.sharding import PartitionSpec as P

SECTIONS = 2
RELAX = 0.8
LANES = 128
F32 = jnp.float32
BF16 = jnp.bfloat16
MESH = pl.DeviceIdType.MESH


def dot(left, right):
    return jnp.dot(left, right, preferred_element_type=F32)


def split(value):
    high = value.astype(BF16)
    return high, (value - high.astype(F32)).astype(BF16)


def smoother(
    n_sector, n_slab, slabs, dof, row,
    iterate, right_side, geometry, scale, rates, index, side, orientation, counts,
    volume_ops, face_ops, time_coupling, precondition,
    smoothed, final_residual,
    cells, cells_low, onehot, edge_onehot, picked, picked_low, partial, edge, masks, face_f32, face_w, volume_f32, volume_w, pre_f32, pre_w,
    residual_parts, source, inverse, rate_rows, closing, state,
    before, after, previous, gain_out, gain_in, offset_out, offset_in,
    send_sems, recv_sems,
):
    count = index.shape[1]
    tiles = count // LANES
    faces = index.shape[0]
    half = count // 2
    width = 3 * count // 8
    my_sector, my_slab = lax.axis_index("sector"), lax.axis_index("slab")
    next_sector = lax.rem(my_sector + 1, n_sector)
    prev_sector = lax.rem(my_sector + n_sector - 1, n_sector)
    ahead = [None] + [lax.rem(my_slab + m, n_slab) for m in range(1, n_slab)]

    barrier = pltpu.get_barrier_semaphore()
    for target in (next_sector, prev_sector):
        pl.semaphore_signal(barrier, inc=1, device_id={"sector": target}, device_id_type=MESH)
    for m in range(1, n_slab):
        pl.semaphore_signal(barrier, inc=1, device_id={"slab": ahead[m]}, device_id_type=MESH)

    def remote(src, dst, slot, target):
        return pltpu.make_async_remote_copy(
            src_ref=src, dst_ref=dst, send_sem=send_sems.at[slot], recv_sem=recv_sems.at[slot],
            device_id=target, device_id_type=MESH,
        )

    per_section = 3 + 2 * (n_slab - 1)
    gain_base = SECTIONS * per_section

    cells[...] = jnp.zeros_like(cells)
    cells_low[...] = jnp.zeros_like(cells_low)

    def lines(s, tile):
        return pl.ds(tile * slabs + s, dof, stride=tiles * slabs), slice(None)

    def load_slab(ref, s, first, stop):
        return jnp.concatenate([ref[lines(s, tile)] for tile in range(first, stop)], axis=1)

    def store_slab(ref, s, value, first):
        for tile in range(value.shape[1] // LANES):
            ref[lines(s, first + tile)] = value[:, tile * LANES : (tile + 1) * LANES]

    def to_cells(s, carry):
        high, low = split(load_slab(iterate, s, 0, tiles))
        cells[s + 1, 0:dof, :] = high
        cells_low[s + 1, 0:dof, :] = low
        return carry

    lax.fori_loop(0, slabs, to_cells, 0)
    total = 1.0 / scale[0:1, :]
    inverse[0:1, :] = total
    for s in range(1, slabs):
        one = 1.0 / scale[s : s + 1, :]
        inverse[s : s + 1, :] = one
        total = total * one
    gain_out[...] = jnp.broadcast_to(total, gain_out.shape)

    pl.semaphore_wait(barrier, 2 + n_slab - 1)

    def field_copies(section):
        base = section * per_section
        inner = cells.at[pl.ds(1, slabs)]
        return [
            remote(inner.at[:, :, pl.ds(half, half)], before.at[section], base, {"sector": next_sector}),
            remote(inner.at[:, :, pl.ds(0, half)], after.at[section], base + 1, {"sector": prev_sector}),
            remote(cells.at[slabs], previous.at[section], base + 2, {"slab": ahead[1]}),
        ]

    def offset_copies(section, part):
        base = section * per_section + 2 + part * (n_slab - 1)
        return [
            remote(offset_out.at[section, part], offset_in.at[section, part, m], base + m, {"slab": ahead[m]})
            for m in range(1, n_slab)
        ]

    gain_copies = [
        remote(gain_out, gain_in.at[m], gain_base + m - 1, {"slab": ahead[m]}) for m in range(1, n_slab)
    ]

    field_now = field_copies(0)
    for copy in field_now:
        copy.start()
    for copy in gain_copies:
        copy.start()

    rows = lax.broadcasted_iota(jnp.int32, (count, count), 0)
    side_first = side[0:1, :]
    index_first = index[0:1, :]
    own_first = jnp.where(side_first == 0, index_first, -1)
    onehot[0] = jnp.where(rows == own_first, 1.0, 0.0).astype(BF16)

    def build(f, carry):
        onehot[f] = jnp.where(rows == index[pl.ds(f, 1), :], 1.0, 0.0).astype(BF16)
        return carry

    lax.fori_loop(1, faces, build, 0)
    edge_rows = lax.broadcasted_iota(jnp.int32, (half, half), 0)
    from_before = jnp.where(side_first < 0, index_first - half, -1)[:, 0:half]
    from_after = jnp.where(side_first > 0, index_first, -1)[:, half:count]
    edge_onehot[0] = jnp.where(edge_rows == from_before, 1.0, 0.0).astype(BF16)
    edge_onehot[1] = jnp.where(edge_rows == from_after, 1.0, 0.0).astype(BF16)
    for f in range(faces):
        turned = orientation[f : f + 1, :]
        for o in range(3):
            mask = jnp.where(turned == o, 1.0, 0.0)
            masks[3 * f + o] = jnp.broadcast_to(mask, (row, count)).astype(BF16)

    face_f32[...] = jnp.zeros_like(face_f32)
    for f in range(faces):
        for o in range(3):
            at = (3 * f + o) * row
            face_f32[0:dof, at : at + dof] = face_ops[f, :, o * dof : (o + 1) * dof]
    high, low = split(face_f32[...])
    face_w[0:row, :] = high
    face_w[row : 2 * row, :] = low
    volume_f32[...] = jnp.zeros_like(volume_f32)
    volume_f32[0:dof, 0:dof] = -time_coupling[...]
    for d in range(4):
        volume_f32[d * row : d * row + dof, row : row + dof] = volume_ops[:, d, :]
    high, low = split(volume_f32[...])
    volume_w[:, 0 : 2 * row] = high
    volume_w[:, 2 * row : 4 * row] = low
    volume_w[:, 4 * row : 6 * row] = high
    pre_f32[...] = jnp.zeros_like(pre_f32)
    for part in range(3):
        pre_f32[0:dof, part * row : part * row + dof] = precondition[...]
    high, low = split(pre_f32[...])
    part_of = lax.broadcasted_iota(jnp.int32, pre_f32.shape, 1) // row
    pre_w[...] = jnp.where(part_of == 1, low.astype(F32), high.astype(F32)).astype(BF16)
    residual_parts[...] = jnp.zeros_like(residual_parts)

    diagonal = lax.broadcasted_iota(jnp.int32, (dof, dof), 0) == lax.broadcasted_iota(jnp.int32, (dof, dof), 1)
    column = jnp.sum(jnp.where(diagonal, jnp.broadcast_to(rates[...], (dof, dof)), 0.0), axis=1, keepdims=True)
    rate_rows[...] = jnp.broadcast_to(column, (dof, count))
    power = column
    for _ in range(slabs - 1):
        power = power * column

    slots = lax.broadcasted_iota(jnp.int32, (1, count), 1)
    live = jnp.where((slots < counts[0] - width) | (slots >= count - width), 1.0, 0.0)
    offset_out[...] = jnp.zeros_like(offset_out)

    for section in range(SECTIONS):
        last = section == SECTIONS - 1
        flat = slabs * row

        def gather(f, carry):
            values = cells[pl.ds(1, slabs)].reshape(flat, count)
            picked[f] = dot(values, onehot[f]).astype(BF16).reshape(slabs, row, count)
            values = cells_low[pl.ds(1, slabs)].reshape(flat, count)
            picked_low[f] = dot(values, onehot[f]).astype(BF16).reshape(slabs, row, count)
            return carry

        lax.fori_loop(0, faces, gather, 0)
        cells[0] = jnp.zeros_like(cells[0])

        def apply(s, carry):
            pair = cells[pl.ds(s, 2)].reshape(2 * row, count)
            pair_low = cells_low[pl.ds(s, 2)].reshape(2 * row, count)
            terms = dot(volume_w[...], jnp.concatenate([pair, pair, pair_low], axis=0))
            applied = terms[0:row]
            for d in range(3):
                applied = applied + geometry[d, pl.ds(s, 1), :] * terms[(d + 1) * row : (d + 2) * row]
            blocks, blocks_low = [], []
            for f in range(faces):
                block, block_low = picked[f, s], picked_low[f, s]
                for o in range(3):
                    blocks.append(block * masks[3 * f + o])
                    blocks_low.append(block_low * masks[3 * f + o])
            flux = dot(face_w[...], jnp.concatenate(blocks, axis=0))
            flux_low = dot(face_w[0:row, :], jnp.concatenate(blocks_low, axis=0))
            partial[s] = applied + flux[0:row] + flux[row : 2 * row] + flux_low
            return carry

        lax.fori_loop(0, slabs, apply, 0, unroll=min(2, slabs))
        for copy in field_now:
            copy.wait()
        slab_before = previous[section]
        weights = jnp.concatenate([volume_w[0:row, 0:row], volume_w[0:row, 2 * row : 3 * row]], axis=1)
        partial[0] = partial[0] + dot(weights, jnp.concatenate([slab_before, slab_before], axis=0))
        left = dot(before[section].reshape(flat, half), edge_onehot[0]).astype(BF16)
        edge[:, :, 0:half] = left.reshape(slabs, row, half)
        right = dot(after[section].reshape(flat, half), edge_onehot[1]).astype(BF16)
        edge[:, :, half:count] = right.reshape(slabs, row, half)
        state[...] = jnp.zeros_like(state)

        offsets = []
        for part in range(2):
            lanes = slice(part * half, (part + 1) * half)
            first, stop = part * tiles // 2, (part + 1) * tiles // 2

            def finish(s, carry):
                block = edge[s, :, lanes]
                crossing = jnp.concatenate([block * masks[o, :, lanes] for o in range(3)], axis=0)
                flux = dot(face_w[:, 0 : 3 * row], crossing)
                applied = partial[s, :, lanes] + flux[0:row] + flux[row : 2 * row]
                residual = live[:, lanes] * (load_slab(right_side, s, first, stop) - applied[0:dof])
                if last:
                    store_slab(final_residual, s, residual, first)
                high, low = split(residual)
                residual_parts[s, 0:dof, lanes] = high
                residual_parts[s, row : row + dof, lanes] = high
                residual_parts[s, 2 * row : 2 * row + dof, lanes] = low
                source[s, 0:dof, lanes] = dot(pre_w[...], residual_parts[s, :, lanes])[0:dof].astype(BF16)
                return carry

            def collect(s, carry):
                state[:, lanes] = inverse[pl.ds(s, 1), lanes] * (
                    rate_rows[:, lanes] * state[:, lanes] + source[s, 0:dof, lanes].astype(F32)
                )
                return carry

            lax.fori_loop(0, slabs, finish, 0, unroll=min(4, slabs))
            lax.fori_loop(0, slabs, collect, 0, unroll=min(2, slabs))
            offset_out[section, part, 0:dof, :] = state[:, lanes].astype(BF16)
            offsets.append(offset_copies(section, part))
            for copy in offsets[part]:
                copy.start()
        if section == 0:
            for copy in gain_copies:
                copy.wait()
            whole = power * gain_out[0:1, :]
            for m in range(1, n_slab):
                whole = whole * (power * gain_in[m, 0:1, :])
            closing[...] = 1.0 / (1.0 - whole)
        field = iterate if section == 0 else smoothed
        if not last:
            field_now = field_copies(section + 1)
        for part in range(2):
            lanes = slice(part * half, (part + 1) * half)
            first, stop = part * tiles // 2, (part + 1) * tiles // 2
            for copy in offsets[part]:
                copy.wait()
            entering = state[:, lanes]
            for m in range(n_slab - 1, 0, -1):
                gain = power * gain_in[m, 0:1, lanes]
                entering = offset_in[section, part, m, 0:dof, :].astype(F32) + gain * entering
            state[:, lanes] = entering * closing[:, lanes]

            def advance(s, carry):
                value = inverse[pl.ds(s, 1), lanes] * (
                    rate_rows[:, lanes] * state[:, lanes] + source[s, 0:dof, lanes].astype(F32)
                )
                state[:, lanes] = value
                updated = load_slab(field, s, first, stop) + RELAX * value.astype(BF16).astype(F32)
                store_slab(smoothed, s, updated, first)
                if not last:
                    high, low = split(updated)
                    cells[s + 1, 0:dof, lanes] = high
                    cells_low[s + 1, 0:dof, lanes] = low
                return carry

            lax.fori_loop(0, slabs, advance, 0, unroll=min(2, slabs))
            if not last:
                for copy in ([field_now[1]] if part == 0 else [field_now[0], field_now[2]]):
                    copy.start()


def on_device(
    n_sector, n_slab,
    iterate, right_side, geometry, temporal_block_scale, decay_rates, neighbour_index,
    neighbour_side, orientation, sector_counts, volume_ops, face_ops, time_coupling, precondition,
):
    slabs, dof, count = iterate.shape
    faces = neighbour_index.shape[0]
    row = -(-dof // 16) * 16
    half = count // 2
    tiles = count // LANES
    vmem = pl.BlockSpec(memory_space=pltpu.VMEM)
    smem = pl.BlockSpec(memory_space=pltpu.SMEM)
    copies = SECTIONS * (3 + 2 * (n_slab - 1)) + n_slab - 1

    def by_dof(value):
        lined = value.transpose(1, 0, 2).reshape(dof, slabs, tiles, LANES)
        return lined.transpose(0, 2, 1, 3).reshape(dof * tiles * slabs, LANES)

    def by_slab(value):
        lined = value.reshape(dof, tiles, slabs, LANES).transpose(0, 2, 1, 3)
        return lined.reshape(dof, slabs, count).transpose(1, 0, 2)

    out = jax.ShapeDtypeStruct((dof * tiles * slabs, LANES), F32)
    results = pl.pallas_call(
        functools.partial(smoother, n_sector, n_slab, slabs, dof, row),
        out_shape=(out, out),
        in_specs=[vmem] * 8 + [smem] + [vmem] * 4,
        out_specs=(vmem, vmem),
        scratch_shapes=[
            pltpu.VMEM((slabs + 1, row, count), BF16),
            pltpu.VMEM((slabs + 1, row, count), BF16),
            pltpu.VMEM((faces, count, count), BF16),
            pltpu.VMEM((2, half, half), BF16),
            pltpu.VMEM((faces, slabs, row, count), BF16),
            pltpu.VMEM((faces, slabs, row, count), BF16),
            pltpu.VMEM((slabs, row, count), F32),
            pltpu.VMEM((slabs, row, count), BF16),
            pltpu.VMEM((3 * faces, row, count), BF16),
            pltpu.VMEM((row, 3 * faces * row), F32),
            pltpu.VMEM((2 * row, 3 * faces * row), BF16),
            pltpu.VMEM((4 * row, 2 * row), F32),
            pltpu.VMEM((4 * row, 6 * row), BF16),
            pltpu.VMEM((row, 3 * row), F32),
            pltpu.VMEM((row, 3 * row), BF16),
            pltpu.VMEM((slabs, 3 * row, count), BF16),
            pltpu.VMEM((slabs, row, count), BF16),
            pltpu.VMEM((slabs, count), F32),
            pltpu.VMEM((dof, count), F32),
            pltpu.VMEM((dof, count), F32),
            pltpu.VMEM((dof, count), F32),
            pltpu.VMEM((SECTIONS, slabs, row, half), BF16),
            pltpu.VMEM((SECTIONS, slabs, row, half), BF16),
            pltpu.VMEM((SECTIONS, row, count), BF16),
            pltpu.VMEM((8, count), F32),
            pltpu.VMEM((n_slab, 8, count), F32),
            pltpu.VMEM((SECTIONS, 2, row, half), BF16),
            pltpu.VMEM((SECTIONS, 2, n_slab, row, half), BF16),
            pltpu.SemaphoreType.DMA((copies,)),
            pltpu.SemaphoreType.DMA((copies,)),
        ],
        compiler_params=pltpu.CompilerParams(
            collective_id=0, has_side_effects=True, vmem_limit_bytes=56 << 20
        ),
    )(
        by_dof(iterate), by_dof(right_side), geometry.transpose(1, 0, 2), temporal_block_scale,
        decay_rates[None, :], neighbour_index, neighbour_side, orientation, sector_counts,
        volume_ops.transpose(1, 0, 2), face_ops, time_coupling, precondition,
    )
    return tuple(by_slab(value) for value in results)


def solution(mesh):
    in_specs = (
        P("slab", None, "sector"),
        P("slab", None, "sector"),
        P("slab", None, "sector"),
        P("slab", "sector"),
        P(),
        P(None, "sector"),
        P(None, "sector"),
        P(None, "sector"),
        P("sector"),
        P(),
        P(),
        P(),
        P(),
    )
    out_specs = (P("slab", None, "sector"), P("slab", None, "sector"))
    body = functools.partial(on_device, mesh.shape["sector"], mesh.shape["slab"])
    return jax.shard_map(body, mesh=mesh, in_specs=in_specs, out_specs=out_specs, check_vma=False)
```
